32 devices in a mesh: inputs: 8 (over z, y), tm: 4 (over x, core).
Axes of the slice: x: 2, y: 2, z: 4, core: 2. Of those that a mesh axis runs over, the one named last changes fastest.
Arguments:
- voltages: bfloat16 [128, 131072], P('inputs', 'tm'), may hold values from -8 to 8
- pfb_taps: float32 [8, 512], replicated, may hold values from -2 to 2
Outputs:
- visibilities: float32 [256, 1, 2, 128, 128], P(('inputs', 'tm'))
The draws below stay inside these ranges and needn't reach their ends.
All inputs are finite; a program needn't handle non-finite values.
Results may differ from the reference program's by a relative error of at most 0.002.
Values may be sent and summed in bfloat16 or wider, within the bound.
No kernel may reach another device: no remote copies, remote signals or barrier semaphores. Data moves between devices by JAX's collectives and lax.ppermute only.
A program may use at most 128 MiB of HBM per device.

```python
import jax
import jax.numpy as jnp
from jax import lax

F = 256
TAPS = 8
TILE = 128
FRAME = 512
INPUTS = 128
FRAMES = 256
SAMPLES = 131072
NT = 1


def draw_voltages(key, part):
    base = jax.random.fold_in(key, 7)
    key_sky, key_gain, key_noise = jax.random.split(base, 3)
    sky = jax.random.normal(key_sky, (1, SAMPLES), jnp.float32)
    gain = jax.random.uniform(key_gain, (INPUTS, 1), jnp.float32, 0.3, 0.9)
    noise = jax.random.normal(key_noise, (INPUTS, SAMPLES), jnp.float32)
    values = gain * sky + noise
    return jnp.clip(values, -8.0, 8.0).astype(jnp.bfloat16)


def centred(rng, shape, scale, reach, held_as=jnp.bfloat16):
    return jnp.clip(scale * jax.random.normal(rng, shape, jnp.float32), -reach, reach).astype(held_as)


def setup_inputs(seed: int = 0) -> dict:
    key_of = jax.random.split(jax.random.key(seed), 3)
    return {
        "voltages": draw_voltages(jax.random.fold_in(key_of[2], 71), 0),
        "pfb_taps": centred(key_of[1], (TAPS, FRAME), TAPS ** -0.5, 2.0, jnp.float32),
    }


def dft_table(chans, length):
    rows = jnp.arange(2 * chans, dtype=jnp.int32)
    freq = rows // 2
    part = rows % 2
    samp = jnp.arange(length, dtype=jnp.int32)
    phase = (freq[:, None] * samp[None, :]) % length
    angle = (2.0 * jnp.pi / length) * phase.astype(jnp.float32)
    vals = jnp.where(part[:, None] == 0, jnp.cos(angle), -jnp.sin(angle))
    return (vals * (1.0 / (length ** 0.5))).astype(jnp.bfloat16)


def channelize(group, pfb_taps, table):
    zeros = jnp.zeros((TILE, TAPS - 1, FRAME), jnp.bfloat16)
    extended = jnp.concatenate([zeros, group], axis=1)
    filtered = jnp.zeros((TILE, FRAMES, FRAME), jnp.float32)
    for tap in range(TAPS):
        filtered = filtered + pfb_taps[tap][None, None, :] * extended[:, tap:tap + FRAMES, :].astype(jnp.float32)
    rounded = lax.optimization_barrier(filtered.astype(jnp.bfloat16)).astype(jnp.float32)
    spec = jnp.einsum("kn,itn->kit", table.astype(jnp.float32), rounded)
    return spec.astype(jnp.bfloat16)


def channel_tiles(spec):
    left = jnp.concatenate([spec[0], spec[1]], axis=-1)
    twisted = jnp.concatenate([spec[1], -spec[0]], axis=-1)
    real_rows = []
    imag_rows = []
    for first in range(NT):
        lo = first * TILE
        cols = left[lo:]
        real_part = jnp.dot(left[lo:lo + TILE], cols.T, preferred_element_type=jnp.float32)
        imag_part = jnp.dot(twisted[lo:lo + TILE], cols.T, preferred_element_type=jnp.float32)
        count = NT - first
        real_rows.append(real_part.reshape(TILE, count, TILE).transpose(1, 0, 2))
        imag_rows.append(imag_part.reshape(TILE, count, TILE).transpose(1, 0, 2))
    real_all = jnp.concatenate(real_rows, axis=0)
    imag_all = jnp.concatenate(imag_rows, axis=0)
    return jnp.stack([real_all, imag_all], axis=1) * (1.0 / FRAMES)


def reference(voltages, pfb_taps):
    table = dft_table(F, FRAME)
    groups = voltages.reshape(NT, TILE, FRAMES, FRAME)
    spectra = lax.map(lambda group: channelize(group, pfb_taps, table), groups)
    spectra = spectra.transpose(1, 0, 2, 3).reshape(F, 2, INPUTS, FRAMES)
    return lax.map(channel_tiles, spectra)
```

```python
import functools, math
import jax
import jax.numpy as jnp
import numpy as np
from jax import lax
from jax.experimental import pallas as pl
from jax.experimental.pallas import tpu as pltpu
from jax.sharding import PartitionSpec as P

F = 256
TAPS = 8
TILE = 128
FRAME = 512
LANES = 128
GROUP = 8


def dft_table(chans, length):
    rows = np.arange(2 * chans)
    part, freq = rows // chans, rows % chans
    samp = np.arange(length)
    phase = freq[:, None] * samp[None, :] % length
    angle = np.float32(2.0 * np.pi / length) * phase.astype(np.float32)
    vals = np.where(part[:, None] == 0, np.cos(angle), -np.sin(angle))
    return jnp.asarray((vals * np.float32(1.0 / length**0.5)).astype(np.float32)).astype(jnp.bfloat16)


def front_kernel(halo_ref, volts_ref, taps_ref, table_ref, out_ref, filt_ref, filtb_ref, spec_ref):
    inp = volts_ref.shape[0]
    frames = volts_ref.shape[1] // FRAME
    chans = table_ref.shape[0] // 2
    nt = (((1,), (1,)), ((), ()))

    def group_of(slab, first, block):
        xs = [slab(g) for g in range(GROUP + TAPS - 1)]
        for t in range(GROUP):
            acc = None
            for tap in range(TAPS):
                term = taps_ref[tap : tap + 1, block : block + LANES] * xs[t + tap]
                acc = term if acc is None else acc + term
            filt_ref[block // LANES, pl.ds(first + t, inp, stride=frames), :] = acc

    for block in range(0, FRAME, LANES):

        def first_slab(g):
            if g < TAPS - 1:
                return halo_ref[:, g * FRAME + block : g * FRAME + block + LANES].astype(jnp.float32)
            at = (g - TAPS + 1) * FRAME + block
            return volts_ref[:, at : at + LANES].astype(jnp.float32)

        group_of(first_slab, 0, block)

        @pl.loop(1, frames // GROUP)
        def _(step):
            def slab(g):
                at = pl.multiple_of((step * GROUP + g - TAPS + 1) * FRAME + block, LANES)
                return volts_ref[:, pl.ds(at, LANES)].astype(jnp.float32)

            group_of(slab, step * GROUP, block)

    for block in range(0, FRAME, LANES):
        filtb_ref[:, block : block + LANES] = filt_ref[block // LANES].astype(jnp.bfloat16)
    low = lax.broadcasted_iota(jnp.int32, (chans, LANES), 1) < frames
    for pair in range(inp // 2):
        cols = filtb_ref[pair * 2 * frames : (pair + 1) * 2 * frames, :]
        both = lax.dot_general(table_ref[...], cols, nt, preferred_element_type=jnp.float32)
        real, imag = both[:chans], both[chans:]
        spec_ref[pl.ds(2 * pair, chans, stride=inp), :] = jnp.where(low, real, pltpu.roll(imag, frames, 1))
        spec_ref[pl.ds(2 * pair + 1, chans, stride=inp), :] = jnp.where(low, pltpu.roll(real, frames, 1), imag)
    out_ref[...] = spec_ref[...].astype(jnp.bfloat16)


def front(halo, volts, taps, table):
    inp = volts.shape[0]
    frames = volts.shape[1] // FRAME
    assert 2 * frames == LANES
    vmem = pl.BlockSpec(memory_space=pltpu.VMEM)
    return pl.pallas_call(
        front_kernel,
        out_shape=jax.ShapeDtypeStruct((F * inp, LANES), jnp.bfloat16),
        in_specs=[vmem] * 4,
        out_specs=vmem,
        scratch_shapes=[
            pltpu.VMEM((FRAME // LANES, inp * frames, LANES), jnp.float32),
            pltpu.VMEM((inp * frames, FRAME), jnp.bfloat16),
            pltpu.VMEM((F * inp, LANES), jnp.float32),
        ],
        name="front",
    )(halo, volts, taps, table)


def tiles_kernel(groups, blocks_time, scale, spec_ref, out_ref):
    inp = spec_ref.shape[2]
    per = TILE // inp
    half = LANES // 2
    nt = (((1,), (1,)), ((), ()))
    sign = jnp.where(lax.broadcasted_iota(jnp.int32, (TILE, LANES), 1) < half, 1.0, -1.0)

    def side(tile):
        cols = []
        for tm in range(blocks_time):
            cols.append(
                jnp.concatenate(
                    [spec_ref[(tile * per + g) * blocks_time + tm, 0] for g in range(per)], axis=0
                )
            )
        return cols

    sides = [side(tile) for tile in range(groups // per)]
    pair = 0
    for a in range(len(sides)):
        left = jnp.concatenate(sides[a], axis=1)
        twisted = jnp.concatenate(
            [(pltpu.roll(c.astype(jnp.float32), half, 1) * sign).astype(jnp.bfloat16) for c in sides[a]], axis=1
        )
        for b in range(a, len(sides)):
            right = jnp.concatenate(sides[b], axis=1)
            real = lax.dot_general(left, right, nt, preferred_element_type=jnp.float32)
            imag = lax.dot_general(twisted, right, nt, preferred_element_type=jnp.float32)
            out_ref[0, pair, 0] = real * scale
            out_ref[0, pair, 1] = imag * scale
            pair += 1


def tile_sums(spec, groups, blocks_time, scale):
    _, chans, inp, _ = spec.shape
    count = groups * inp // TILE
    pairs = count * (count + 1) // 2
    return pl.pallas_call(
        functools.partial(tiles_kernel, groups, blocks_time, scale),
        out_shape=jax.ShapeDtypeStruct((chans, pairs, 2, TILE, TILE), jnp.float32),
        grid=(chans,),
        in_specs=[pl.BlockSpec((groups * blocks_time, 1, inp, LANES), lambda c: (0, c, 0, 0))],
        out_specs=pl.BlockSpec((1, pairs, 2, TILE, TILE), lambda c: (c, 0, 0, 0, 0)),
        name="tiles",
    )(spec)


def on_device(voltages, pfb_taps):
    inp = voltages.shape[0]
    frames = voltages.shape[1] // FRAME
    groups, blocks_time = lax.axis_size("inputs"), lax.axis_size("tm")
    tail = voltages[:, voltages.shape[1] - (TAPS - 1) * FRAME :]
    halo = lax.ppermute(tail, "tm", [(i, i + 1) for i in range(blocks_time - 1)])
    spec = front(halo, voltages, pfb_taps, dft_table(F, FRAME))
    turned = lax.all_to_all(spec, ("inputs", "tm"), split_axis=0, concat_axis=0, tiled=True)
    scale = 1.0 / (frames * blocks_time)
    every = groups * blocks_time
    return tile_sums(turned.reshape(every, F // every, inp, LANES), groups, blocks_time, scale)


def solution(mesh):
    return jax.shard_map(
        on_device,
        mesh=mesh,
        in_specs=(P("inputs", "tm"), P()),
        out_specs=P(("inputs", "tm"), None, None, None, None),
        check_vma=False,
    )
```

```python
import functools

import jax
import jax.numpy as jnp
import numpy as np
from jax import lax
from jax.experimental import pallas as pl
from jax.experimental.pallas import tpu as pltpu
from jax.sharding import PartitionSpec as P

F = 256
TAPS = 8
TILE = 128
FRAME = 512
LANES = 128
GROUP = 8
LEAD = 16
WIDE = 4
NT = (((1,), (1,)), ((), ()))
VMEM = pl.BlockSpec(memory_space=pltpu.VMEM)
ANY = pl.BlockSpec(memory_space=pl.ANY)


def params(mib):
    return pltpu.CompilerParams(vmem_limit_bytes=mib << 20)


def dft_table(chans, length):
    phase = np.arange(chans)[:, None] * np.arange(length)[None, :] % length
    angle = np.float32(2.0 * np.pi / length) * phase.astype(np.float32)
    both = np.concatenate([np.cos(angle), -np.sin(angle)]) * np.float32(1.0 / length**0.5)
    return jnp.asarray(both.astype(np.float32)).astype(jnp.bfloat16)


def filter_group(slab, first, block, taps_ref, filt_ref, pitch):
    xs = [slab(g) for g in range(GROUP + TAPS - 1)]
    for t in range(GROUP):
        acc = None
        for tap in range(TAPS):
            term = taps_ref[tap : tap + 1, block : block + LANES] * xs[t + tap]
            acc = term if acc is None else acc + term
        filt_ref[block // LANES, pl.ds(first + t, xs[0].shape[0], stride=pitch), :] = acc


def later_kernel(volts_ref, taps_ref, out_ref, filt_ref):
    inp, frames = volts_ref.shape[0], volts_ref.shape[1] // FRAME
    pitch = filt_ref.shape[1] // inp
    for block in range(0, FRAME, LANES):

        @pl.loop(LEAD // GROUP, frames // GROUP)
        def _(step):
            def slab(g):
                at = pl.multiple_of((step * GROUP + g - TAPS + 1) * FRAME + block, LANES)
                return volts_ref[:, pl.ds(at, LANES)].astype(jnp.float32)

            filter_group(slab, step * GROUP, block, taps_ref, filt_ref, pitch)

        for i in range(inp):
            out_ref[i * frames + LEAD : (i + 1) * frames, block : block + LANES] = filt_ref[
                block // LANES, i * pitch + LEAD : i * pitch + frames, :
            ].astype(jnp.bfloat16)


def later(volts, taps):
    inp, frames = volts.shape[0], volts.shape[1] // FRAME
    return pl.pallas_call(
        later_kernel,
        out_shape=jax.ShapeDtypeStruct((inp * frames, FRAME), jnp.bfloat16),
        in_specs=[VMEM, VMEM],
        out_specs=VMEM,
        scratch_shapes=[pltpu.VMEM((FRAME // LANES, inp * (frames + 8), LANES), jnp.float32)],
        compiler_params=params(12),
        cost_estimate=pl.CostEstimate(flops=16 * inp * frames * FRAME, bytes_accessed=1 << 21, transcendentals=0),
        name="later",
    )(volts, taps)


def transform(filtb_ref, table, out_ref, spec_ref, inp):
    frames = filtb_ref.shape[0] // inp
    chans = table.shape[0] // 2
    pitch = spec_ref.shape[0] // chans
    low = lax.broadcasted_iota(jnp.int32, (chans, LANES), 1) < frames
    for quad in range(0, inp, WIDE):
        cols = filtb_ref[quad * frames : (quad + WIDE) * frames, :]
        both = lax.dot_general(table, cols, NT, preferred_element_type=jnp.float32)
        for p in range(WIDE // 2):
            real, imag = (both[c * chans : (c + 1) * chans, p * LANES : (p + 1) * LANES] for c in (0, 1))
            at = quad + 2 * p
            spec_ref[pl.ds(at, chans, stride=pitch), :] = jnp.where(low, real, pltpu.roll(imag, frames, 1))
            spec_ref[pl.ds(at + 1, chans, stride=pitch), :] = jnp.where(low, pltpu.roll(real, frames, 1), imag)
    for k in range(chans):
        out_ref[k * inp : (k + 1) * inp, :] = spec_ref[k * pitch : k * pitch + inp, :].astype(jnp.bfloat16)


def front_kernel(later_ref, halo_ref, head_ref, taps_ref, table_ref, out_ref, filtb_ref, filt_ref, spec_ref, sem):
    inp = head_ref.shape[0]
    frames = filtb_ref.shape[0] // inp
    copy = pltpu.make_async_copy(later_ref, filtb_ref, sem)
    copy.start()
    for block in range(0, FRAME, LANES):
        for first in range(0, LEAD, GROUP):

            def slab(g):
                t = first + g - (TAPS - 1)
                ref, at = (halo_ref, t + TAPS - 1) if t < 0 else (head_ref, t)
                return ref[:, at * FRAME + block : at * FRAME + block + LANES].astype(jnp.float32)

            filter_group(slab, first, block, taps_ref, filt_ref, filt_ref.shape[1] // inp)
    copy.wait()
    pitch = filt_ref.shape[1] // inp
    for block in range(0, FRAME, LANES):
        for i in range(inp):
            filtb_ref[i * frames : i * frames + LEAD, block : block + LANES] = filt_ref[
                block // LANES, i * pitch : i * pitch + LEAD, :
            ].astype(jnp.bfloat16)
    transform(filtb_ref, table_ref[...], out_ref, spec_ref, inp)


def front(filtered, halo, volts, taps, table):
    inp = volts.shape[0]
    frames = volts.shape[1] // FRAME
    assert 2 * frames == LANES
    chans = table.shape[0] // 2
    return pl.pallas_call(
        front_kernel,
        grid=(1,),
        out_shape=jax.ShapeDtypeStruct((chans * inp, LANES), jnp.bfloat16),
        in_specs=[ANY, VMEM, pl.BlockSpec((inp, LEAD * FRAME), lambda i: (0, 0)), VMEM, VMEM],
        out_specs=VMEM,
        scratch_shapes=[
            pltpu.VMEM(filtered.shape, jnp.bfloat16),
            pltpu.VMEM((FRAME // LANES, inp * (LEAD + 8), LANES), jnp.float32),
            pltpu.VMEM((chans * (inp + 8), LANES), jnp.float32),
            pltpu.SemaphoreType.DMA,
        ],
        compiler_params=params(16),
        name="front",
    )(filtered, halo, volts, taps, table)


def tiles_kernel(groups, blocks_time, scale, spec_ref, out_ref):
    chan = pl.program_id(0)
    per = TILE // spec_ref.shape[2]
    half = LANES // 2
    sign = jnp.where(lax.broadcasted_iota(jnp.int32, (TILE, LANES), 1) < half, 1.0, -1.0)

    def side(tile):
        return [
            jnp.concatenate([spec_ref[(tile * per + g) * blocks_time + tm, chan] for g in range(per)], axis=0)
            for tm in range(blocks_time)
        ]

    pair = 0
    for a in range(groups // per):
        cols = side(a)
        left = jnp.concatenate(cols, axis=1)
        twisted = jnp.concatenate(
            [(pltpu.roll(c.astype(jnp.float32), half, 1) * sign).astype(jnp.bfloat16) for c in cols], axis=1
        )
        for b in range(a, groups // per):
            right = left if b == a else jnp.concatenate(side(b), axis=1)
            out_ref[0, pair, 0] = lax.dot_general(left, right, NT, preferred_element_type=jnp.float32) * scale
            out_ref[0, pair, 1] = lax.dot_general(twisted, right, NT, preferred_element_type=jnp.float32) * scale
            pair += 1


def tile_sums(spec, groups, blocks_time, scale):
    _, chans, inp, _ = spec.shape
    count = groups * inp // TILE
    pairs = count * (count + 1) // 2
    return pl.pallas_call(
        functools.partial(tiles_kernel, groups, blocks_time, scale),
        out_shape=jax.ShapeDtypeStruct((chans, pairs, 2, TILE, TILE), jnp.float32),
        grid=(chans,),
        in_specs=[pl.BlockSpec(spec.shape, lambda c: (0, 0, 0, 0))],
        out_specs=pl.BlockSpec((1, pairs, 2, TILE, TILE), lambda c: (c, 0, 0, 0, 0)),
        compiler_params=params(32),
        name="tiles",
    )(spec)


def on_device(voltages, pfb_taps):
    inp = voltages.shape[0]
    frames = voltages.shape[1] // FRAME
    groups, blocks_time = lax.axis_size("inputs"), lax.axis_size("tm")
    tail = voltages[:, voltages.shape[1] - (TAPS - 1) * FRAME :]
    halo = lax.ppermute(tail, "tm", [(i, i + 1) for i in range(blocks_time - 1)])
    filtered = later(voltages, pfb_taps)
    spec = front(filtered, halo, voltages, pfb_taps, dft_table(F, FRAME))
    turned = lax.all_to_all(spec, ("inputs", "tm"), split_axis=0, concat_axis=0, tiled=True)
    scale = 1.0 / (frames * blocks_time)
    every = groups * blocks_time
    return tile_sums(turned.reshape(every, F // every, inp, LANES), groups, blocks_time, scale)


def solution(mesh):
    return jax.shard_map(
        on_device,
        mesh=mesh,
        in_specs=(P("inputs", "tm"), P()),
        out_specs=P(("inputs", "tm"), None, None, None, None),
        check_vma=False,
    )
```

```python
import functools

import jax
import jax.numpy as jnp
import numpy as np
from jax import lax
from jax.experimental import pallas as pl
from jax.experimental.pallas import tpu as pltpu
from jax.sharding import PartitionSpec as P

F = 256
TAPS = 8
TILE = 128
FRAME = 512
LANES = 128
GROUP = 8
LEAD = 16
WIDE = 4
NT = (((1,), (1,)), ((), ()))
VMEM = pl.BlockSpec(memory_space=pltpu.VMEM)
ANY = pl.BlockSpec(memory_space=pl.ANY)


def params(mib):
    return pltpu.CompilerParams(vmem_limit_bytes=mib << 20)


def dft_table(chans, length):
    phase = np.arange(chans)[:, None] * np.arange(length)[None, :] % length
    angle = np.float32(2.0 * np.pi / length) * phase.astype(np.float32)
    both = np.concatenate([np.cos(angle), -np.sin(angle)]) * np.float32(1.0 / length**0.5)
    return jnp.asarray(both.astype(np.float32)).astype(jnp.bfloat16)


def filter_group(slab, first, block, taps_ref, filt_ref, pitch):
    xs = [slab(g) for g in range(GROUP + TAPS - 1)]
    for t in range(GROUP):
        acc = None
        for tap in range(TAPS):
            term = taps_ref[tap : tap + 1, block : block + LANES] * xs[t + tap]
            acc = term if acc is None else acc + term
        filt_ref[block // LANES, pl.ds(first + t, xs[0].shape[0], stride=pitch), :] = acc


def tail_kernel(volts_ref, tail_ref, sem):
    span = tail_ref.shape[1]
    copy = pltpu.make_async_copy(volts_ref.at[:, pl.ds(volts_ref.shape[1] - span, span)], tail_ref, sem)
    copy.start()
    copy.wait()


def last_frames(volts):
    return pl.pallas_call(
        tail_kernel,
        out_shape=jax.ShapeDtypeStruct((volts.shape[0], (TAPS - 1) * FRAME), volts.dtype),
        in_specs=[ANY],
        out_specs=VMEM,
        scratch_shapes=[pltpu.SemaphoreType.DMA],
        compiler_params=params(62),
        name="tail",
    )(volts)


def later_kernel(volts_ref, taps_ref, out_ref, filt_ref):
    inp, frames = volts_ref.shape[0], volts_ref.shape[1] // FRAME
    pitch = filt_ref.shape[1] // inp
    for block in range(0, FRAME, LANES):

        @pl.loop(LEAD // GROUP, frames // GROUP)
        def _(step):
            def slab(g):
                at = pl.multiple_of((step * GROUP + g - TAPS + 1) * FRAME + block, LANES)
                return volts_ref[:, pl.ds(at, LANES)].astype(jnp.float32)

            filter_group(slab, step * GROUP, block, taps_ref, filt_ref, pitch)

        for i in range(inp):
            out_ref[i * frames + LEAD : (i + 1) * frames, block : block + LANES] = filt_ref[
                block // LANES, i * pitch + LEAD : i * pitch + frames, :
            ].astype(jnp.bfloat16)


def later(volts, taps):
    inp, frames = volts.shape[0], volts.shape[1] // FRAME
    return pl.pallas_call(
        later_kernel,
        out_shape=jax.ShapeDtypeStruct((inp * frames, FRAME), jnp.bfloat16),
        in_specs=[VMEM, VMEM],
        out_specs=VMEM,
        scratch_shapes=[pltpu.VMEM((FRAME // LANES, inp * (frames + 8), LANES), jnp.float32)],
        compiler_params=params(12),
        cost_estimate=pl.CostEstimate(flops=16 * inp * frames * FRAME, bytes_accessed=1 << 21, transcendentals=0),
        name="later",
    )(volts, taps)


def transform(filtb_ref, table, out_ref, spec_ref, inp):
    frames = filtb_ref.shape[0] // inp
    chans = table.shape[0] // 2
    pitch = spec_ref.shape[0] // chans
    low = lax.broadcasted_iota(jnp.int32, (chans, LANES), 1) < frames
    for quad in range(0, inp, WIDE):
        cols = filtb_ref[quad * frames : (quad + WIDE) * frames, :]
        both = lax.dot_general(table, cols, NT, preferred_element_type=jnp.float32)
        for p in range(WIDE // 2):
            real, imag = (both[c * chans : (c + 1) * chans, p * LANES : (p + 1) * LANES] for c in (0, 1))
            at = quad + 2 * p
            spec_ref[pl.ds(at, chans, stride=pitch), :] = jnp.where(low, real, pltpu.roll(imag, frames, 1))
            spec_ref[pl.ds(at + 1, chans, stride=pitch), :] = jnp.where(low, pltpu.roll(real, frames, 1), imag)
    for k in range(chans):
        out_ref[k * inp : (k + 1) * inp, :] = spec_ref[k * pitch : k * pitch + inp, :].astype(jnp.bfloat16)


def front_kernel(later_ref, halo_ref, head_ref, taps_ref, table_ref, out_ref, filtb_ref, filt_ref, spec_ref, sem):
    inp = head_ref.shape[0]
    frames = filtb_ref.shape[0] // inp
    copy = pltpu.make_async_copy(later_ref, filtb_ref, sem)
    copy.start()
    for block in range(0, FRAME, LANES):
        for first in range(0, LEAD, GROUP):

            def slab(g):
                t = first + g - (TAPS - 1)
                ref, at = (halo_ref, t + TAPS - 1) if t < 0 else (head_ref, t)
                return ref[:, at * FRAME + block : at * FRAME + block + LANES].astype(jnp.float32)

            filter_group(slab, first, block, taps_ref, filt_ref, filt_ref.shape[1] // inp)
    copy.wait()
    pitch = filt_ref.shape[1] // inp
    for block in range(0, FRAME, LANES):
        for i in range(inp):
            filtb_ref[i * frames : i * frames + LEAD, block : block + LANES] = filt_ref[
                block // LANES, i * pitch : i * pitch + LEAD, :
            ].astype(jnp.bfloat16)
    transform(filtb_ref, table_ref[...], out_ref, spec_ref, inp)


def front(filtered, halo, volts, taps, table):
    inp = volts.shape[0]
    frames = volts.shape[1] // FRAME
    assert 2 * frames == LANES
    chans = table.shape[0] // 2
    return pl.pallas_call(
        front_kernel,
        out_shape=jax.ShapeDtypeStruct((chans * inp, LANES), jnp.bfloat16),
        in_specs=[ANY, VMEM, VMEM, VMEM, VMEM],
        out_specs=VMEM,
        scratch_shapes=[
            pltpu.VMEM(filtered.shape, jnp.bfloat16),
            pltpu.VMEM((FRAME // LANES, inp * (LEAD + 8), LANES), jnp.float32),
            pltpu.VMEM((chans * (inp + 8), LANES), jnp.float32),
            pltpu.SemaphoreType.DMA,
        ],
        compiler_params=params(16),
        name="front",
    )(filtered, halo, volts, taps, table)


def tiles_kernel(groups, blocks_time, scale, spec_ref, out_ref):
    chan = pl.program_id(0)
    per = TILE // spec_ref.shape[2]
    half = LANES // 2
    sign = jnp.where(lax.broadcasted_iota(jnp.int32, (TILE, LANES), 1) < half, 1.0, -1.0)

    def side(tile):
        return [
            jnp.concatenate([spec_ref[(tile * per + g) * blocks_time + tm, chan] for g in range(per)], axis=0)
            for tm in range(blocks_time)
        ]

    pair = 0
    for a in range(groups // per):
        cols = side(a)
        left = jnp.concatenate(cols, axis=1)
        twisted = jnp.concatenate(
            [(pltpu.roll(c.astype(jnp.float32), half, 1) * sign).astype(jnp.bfloat16) for c in cols], axis=1
        )
        for b in range(a, groups // per):
            right = left if b == a else jnp.concatenate(side(b), axis=1)
            out_ref[0, pair, 0] = lax.dot_general(left, right, NT, preferred_element_type=jnp.float32) * scale
            out_ref[0, pair, 1] = lax.dot_general(twisted, right, NT, preferred_element_type=jnp.float32) * scale
            pair += 1


def tile_sums(spec, groups, blocks_time, scale):
    _, chans, inp, _ = spec.shape
    count = groups * inp // TILE
    pairs = count * (count + 1) // 2
    return pl.pallas_call(
        functools.partial(tiles_kernel, groups, blocks_time, scale),
        out_shape=jax.ShapeDtypeStruct((chans, pairs, 2, TILE, TILE), jnp.float32),
        grid=(chans,),
        in_specs=[VMEM],
        out_specs=pl.BlockSpec((1, pairs, 2, TILE, TILE), lambda c: (c, 0, 0, 0, 0)),
        compiler_params=params(32),
        name="tiles",
    )(spec)


def on_device(voltages, pfb_taps):
    inp = voltages.shape[0]
    frames = voltages.shape[1] // FRAME
    groups, blocks_time = lax.axis_size("inputs"), lax.axis_size("tm")
    tail = last_frames(voltages)
    halo = lax.ppermute(tail, "tm", [(i, i + 1) for i in range(blocks_time - 1)])
    filtered = later(voltages, pfb_taps)
    spec = front(filtered, halo, voltages, pfb_taps, dft_table(F, FRAME))
    turned = lax.all_to_all(spec, ("inputs", "tm"), split_axis=0, concat_axis=0, tiled=True)
    scale = 1.0 / (frames * blocks_time)
    every = groups * blocks_time
    return tile_sums(turned.reshape(every, F // every, inp, LANES), groups, blocks_time, scale)


def solution(mesh):
    return jax.shard_map(
        on_device,
        mesh=mesh,
        in_specs=(P("inputs", "tm"), P()),
        out_specs=P(("inputs", "tm"), None, None, None, None),
        check_vma=False,
    )
```

```python
import functools

import jax
import jax.numpy as jnp
import numpy as np
from jax import lax
from jax.experimental import pallas as pl
from jax.experimental.pallas import tpu as pltpu
from jax.sharding import PartitionSpec as P

F = 256
TAPS = 8
TILE = 128
FRAME = 512
LANES = 128
GROUP = 8
LEAD = 16
WIDE = 4
NT = (((1,), (1,)), ((), ()))
VMEM = pl.BlockSpec(memory_space=pltpu.VMEM)
ANY = pl.BlockSpec(memory_space=pl.ANY)


def params(mib):
    return pltpu.CompilerParams(vmem_limit_bytes=mib << 20)


def dft_table(chans, length):
    phase = np.arange(chans)[:, None] * np.arange(length)[None, :] % length
    angle = np.float32(2.0 * np.pi / length) * phase.astype(np.float32)
    both = np.concatenate([np.cos(angle), -np.sin(angle)]) * np.float32(1.0 / length**0.5)
    return jnp.asarray(both.astype(np.float32)).astype(jnp.bfloat16)


def filter_group(slab, first, block, taps_ref, filt_ref, pitch):
    xs = [slab(g) for g in range(GROUP + TAPS - 1)]
    for t in range(GROUP):
        acc = None
        for tap in range(TAPS):
            term = taps_ref[tap : tap + 1, block : block + LANES] * xs[t + tap]
            acc = term if acc is None else acc + term
        filt_ref[block // LANES, pl.ds(first + t, xs[0].shape[0], stride=pitch), :] = acc


def later_kernel(volts_ref, taps_ref, out_ref, filt_ref):
    inp, frames = volts_ref.shape[0], volts_ref.shape[1] // FRAME
    pitch = filt_ref.shape[1] // inp
    for block in range(0, FRAME, LANES):

        @pl.loop(LEAD // GROUP, frames // GROUP)
        def _(step):
            def slab(g):
                at = pl.multiple_of((step * GROUP + g - TAPS + 1) * FRAME + block, LANES)
                return volts_ref[:, pl.ds(at, LANES)].astype(jnp.float32)

            filter_group(slab, step * GROUP, block, taps_ref, filt_ref, pitch)

        for i in range(inp):
            out_ref[i * frames + LEAD : (i + 1) * frames, block : block + LANES] = filt_ref[
                block // LANES, i * pitch + LEAD : i * pitch + frames, :
            ].astype(jnp.bfloat16)


def later(volts, taps):
    inp, frames = volts.shape[0], volts.shape[1] // FRAME
    return pl.pallas_call(
        later_kernel,
        out_shape=jax.ShapeDtypeStruct((inp * frames, FRAME), jnp.bfloat16),
        in_specs=[VMEM, VMEM],
        out_specs=VMEM,
        scratch_shapes=[pltpu.VMEM((FRAME // LANES, inp * (frames + 8), LANES), jnp.float32)],
        compiler_params=params(12),
        cost_estimate=pl.CostEstimate(flops=16 * inp * frames * FRAME, bytes_accessed=1 << 21, transcendentals=0),
        name="later",
    )(volts, taps)


def transform(filtb_ref, table, out_ref, spec_ref, inp):
    frames = filtb_ref.shape[0] // inp
    chans = table.shape[0] // 2
    pitch = spec_ref.shape[0] // chans
    low = lax.broadcasted_iota(jnp.int32, (chans, LANES), 1) < frames
    for quad in range(0, inp, WIDE):
        cols = filtb_ref[quad * frames : (quad + WIDE) * frames, :]
        both = lax.dot_general(table, cols, NT, preferred_element_type=jnp.float32)
        for p in range(WIDE // 2):
            real, imag = (both[c * chans : (c + 1) * chans, p * LANES : (p + 1) * LANES] for c in (0, 1))
            at = quad + 2 * p
            spec_ref[pl.ds(at, chans, stride=pitch), :] = jnp.where(low, real, pltpu.roll(imag, frames, 1))
            spec_ref[pl.ds(at + 1, chans, stride=pitch), :] = jnp.where(low, pltpu.roll(real, frames, 1), imag)
    for k in range(chans):
        out_ref[k * inp : (k + 1) * inp, :] = spec_ref[k * pitch : k * pitch + inp, :].astype(jnp.bfloat16)


def front_kernel(later_ref, halo_ref, head_ref, taps_ref, table_ref, out_ref, filtb_ref, filt_ref, spec_ref, sem):
    inp = head_ref.shape[0]
    frames = filtb_ref.shape[0] // inp
    copy = pltpu.make_async_copy(later_ref, filtb_ref, sem)
    copy.start()
    for block in range(0, FRAME, LANES):
        for first in range(0, LEAD, GROUP):

            def slab(g):
                t = first + g - (TAPS - 1)
                ref, at = (halo_ref, t + TAPS - 1) if t < 0 else (head_ref, t)
                return ref[:, at * FRAME + block : at * FRAME + block + LANES].astype(jnp.float32)

            filter_group(slab, first, block, taps_ref, filt_ref, filt_ref.shape[1] // inp)
    copy.wait()
    pitch = filt_ref.shape[1] // inp
    for block in range(0, FRAME, LANES):
        for i in range(inp):
            filtb_ref[i * frames : i * frames + LEAD, block : block + LANES] = filt_ref[
                block // LANES, i * pitch : i * pitch + LEAD, :
            ].astype(jnp.bfloat16)
    transform(filtb_ref, table_ref[...], out_ref, spec_ref, inp)


def front(filtered, halo, volts, taps, table):
    inp = volts.shape[0]
    frames = volts.shape[1] // FRAME
    assert 2 * frames == LANES
    chans = table.shape[0] // 2
    return pl.pallas_call(
        front_kernel,
        out_shape=jax.ShapeDtypeStruct((chans * inp, LANES), jnp.bfloat16),
        in_specs=[ANY, VMEM, VMEM, VMEM, VMEM],
        out_specs=VMEM,
        scratch_shapes=[
            pltpu.VMEM(filtered.shape, jnp.bfloat16),
            pltpu.VMEM((FRAME // LANES, inp * (LEAD + 8), LANES), jnp.float32),
            pltpu.VMEM((chans * (inp + 8), LANES), jnp.float32),
            pltpu.SemaphoreType.DMA,
        ],
        compiler_params=params(16),
        name="front",
    )(filtered, halo, volts, taps, table)


def tiles_kernel(groups, blocks_time, scale, spec_ref, out_ref, held_ref, sem):
    per = TILE // spec_ref.shape[2]
    half = LANES // 2
    sign = jnp.where(lax.broadcasted_iota(jnp.int32, (TILE, LANES), 1) < half, 1.0, -1.0)
    copies = []
    for chan in range(spec_ref.shape[1]):

        def side(tile):
            return [
                jnp.concatenate([spec_ref[(tile * per + g) * blocks_time + tm, chan] for g in range(per)], axis=0)
                for tm in range(blocks_time)
            ]

        pair = 0
        for a in range(groups // per):
            cols = side(a)
            left = jnp.concatenate(cols, axis=1)
            twisted = jnp.concatenate(
                [(pltpu.roll(c.astype(jnp.float32), half, 1) * sign).astype(jnp.bfloat16) for c in cols], axis=1
            )
            for b in range(a, groups // per):
                right = left if b == a else jnp.concatenate(side(b), axis=1)
                for part, mine in enumerate((left, twisted)):
                    sums = lax.dot_general(mine, right, NT, preferred_element_type=jnp.float32)
                    held_ref[chan, pair, part] = sums * scale
                pair += 1
        copies.append(pltpu.make_async_copy(held_ref.at[chan], out_ref.at[chan], sem.at[chan]))
        copies[-1].start()
    for copy in copies:
        copy.wait()


def tile_sums(spec, groups, blocks_time, scale):
    _, chans, inp, _ = spec.shape
    count = groups * inp // TILE
    shape = (chans, count * (count + 1) // 2, 2, TILE, TILE)
    return pl.pallas_call(
        functools.partial(tiles_kernel, groups, blocks_time, scale),
        out_shape=jax.ShapeDtypeStruct(shape, jnp.float32),
        in_specs=[VMEM],
        out_specs=ANY,
        scratch_shapes=[pltpu.VMEM(shape, jnp.float32), pltpu.SemaphoreType.DMA((chans,))],
        compiler_params=params(32),
        name="tiles",
    )(spec)


def on_device(voltages, pfb_taps):
    inp = voltages.shape[0]
    frames = voltages.shape[1] // FRAME
    groups, blocks_time = lax.axis_size("inputs"), lax.axis_size("tm")
    tail = voltages[:, voltages.shape[1] - (TAPS - 1) * FRAME :]
    halo = lax.ppermute(tail, "tm", [(i, i + 1) for i in range(blocks_time - 1)])
    filtered = later(voltages, pfb_taps)
    spec = front(filtered, halo, voltages, pfb_taps, dft_table(F, FRAME))
    turned = lax.all_to_all(spec, ("inputs", "tm"), split_axis=0, concat_axis=0, tiled=True)
    scale = 1.0 / (frames * blocks_time)
    every = groups * blocks_time
    return tile_sums(turned.reshape(every, F // every, inp, LANES), groups, blocks_time, scale)


def solution(mesh):
    return jax.shard_map(
        on_device,
        mesh=mesh,
        in_specs=(P("inputs", "tm"), P()),
        out_specs=P(("inputs", "tm"), None, None, None, None),
        check_vma=False,
    )
```

```python
import functools

import jax
import jax.numpy as jnp
import numpy as np
from jax import lax
from jax.experimental import pallas as pl
from jax.experimental.pallas import tpu as pltpu
from jax.sharding import PartitionSpec as P

F = 256
TAPS = 8
TILE = 128
FRAME = 512
LANES = 128
GROUP = 8
LEAD = 16
WIDE = 4
NT = (((1,), (1,)), ((), ()))
VMEM = pl.BlockSpec(memory_space=pltpu.VMEM)
ANY = pl.BlockSpec(memory_space=pl.ANY)


def params(mib):
    return pltpu.CompilerParams(vmem_limit_bytes=mib << 20)


def dft_table(chans, length):
    phase = np.arange(chans)[:, None] * np.arange(length)[None, :] % length
    angle = np.float32(2.0 * np.pi / length) * phase.astype(np.float32)
    both = np.concatenate([np.cos(angle), -np.sin(angle)]) * np.float32(1.0 / length**0.5)
    return jnp.asarray(both.astype(np.float32)).astype(jnp.bfloat16)


def filter_group(slab, first, block, taps_ref, filt_ref, pitch):
    xs = [slab(g) for g in range(GROUP + TAPS - 1)]
    for t in range(GROUP):
        acc = None
        for tap in range(TAPS):
            term = taps_ref[tap : tap + 1, block : block + LANES] * xs[t + tap]
            acc = term if acc is None else acc + term
        filt_ref[block // LANES, pl.ds(first + t, xs[0].shape[0], stride=pitch), :] = acc


def later_kernel(volts_ref, taps_ref, out_ref, head_ref, filt_ref):
    inp, frames = volts_ref.shape[0], volts_ref.shape[1] // FRAME
    pitch = filt_ref.shape[1] // inp
    head_ref[...] = volts_ref[:, : LEAD * FRAME]
    for block in range(0, FRAME, LANES):

        @pl.loop(LEAD // GROUP, frames // GROUP)
        def _(step):
            def slab(g):
                at = pl.multiple_of((step * GROUP + g - TAPS + 1) * FRAME + block, LANES)
                return volts_ref[:, pl.ds(at, LANES)].astype(jnp.float32)

            filter_group(slab, step * GROUP, block, taps_ref, filt_ref, pitch)

        for i in range(inp):
            out_ref[i * frames + LEAD : (i + 1) * frames, block : block + LANES] = filt_ref[
                block // LANES, i * pitch + LEAD : i * pitch + frames, :
            ].astype(jnp.bfloat16)


def later(volts, taps):
    inp, frames = volts.shape[0], volts.shape[1] // FRAME
    return pl.pallas_call(
        later_kernel,
        out_shape=[
            jax.ShapeDtypeStruct((inp * frames, FRAME), jnp.bfloat16),
            jax.ShapeDtypeStruct((inp, LEAD * FRAME), volts.dtype),
        ],
        in_specs=[VMEM, VMEM],
        out_specs=[VMEM, VMEM],
        scratch_shapes=[pltpu.VMEM((FRAME // LANES, inp * (frames + 8), LANES), jnp.float32)],
        compiler_params=params(12),
        cost_estimate=pl.CostEstimate(flops=16 * inp * frames * FRAME, bytes_accessed=1 << 21, transcendentals=0),
        name="later",
    )(volts, taps)


def transform(columns, table, out_ref, spec_ref, inp, frames):
    chans = table.shape[0] // 2
    pitch = spec_ref.shape[0] // chans
    low = lax.broadcasted_iota(jnp.int32, (chans, LANES), 1) < frames
    for quad in range(0, inp, WIDE):
        cols = jnp.concatenate([columns(i) for i in range(quad, quad + WIDE)], axis=0)
        both = lax.dot_general(table, cols, NT, preferred_element_type=jnp.float32)
        for p in range(WIDE // 2):
            real, imag = (both[c * chans : (c + 1) * chans, p * LANES : (p + 1) * LANES] for c in (0, 1))
            at = quad + 2 * p
            spec_ref[pl.ds(at, chans, stride=pitch), :] = jnp.where(low, real, pltpu.roll(imag, frames, 1))
            spec_ref[pl.ds(at + 1, chans, stride=pitch), :] = jnp.where(low, pltpu.roll(real, frames, 1), imag)
    for k in range(chans):
        out_ref[k * inp : (k + 1) * inp, :] = spec_ref[k * pitch : k * pitch + inp, :].astype(jnp.bfloat16)


def front_kernel(later_ref, halo_ref, head_ref, taps_ref, table_ref, out_ref, filt_ref, spec_ref):
    inp = head_ref.shape[0]
    frames = later_ref.shape[0] // inp
    pitch = filt_ref.shape[1] // inp
    follows = lax.axis_index("tm") > 0
    for block in range(0, FRAME, LANES):
        for first in range(0, LEAD, GROUP):

            def slab(g):
                t = first + g - (TAPS - 1)
                ref, at = (halo_ref, t + TAPS - 1) if t < 0 else (head_ref, t)
                held = ref[:, at * FRAME + block : at * FRAME + block + LANES].astype(jnp.float32)
                return held if t >= 0 else jnp.where(follows, held, 0.0)

            filter_group(slab, first, block, taps_ref, filt_ref, pitch)

    def columns(i):
        lead = [filt_ref[b, i * pitch : i * pitch + LEAD, :].astype(jnp.bfloat16) for b in range(FRAME // LANES)]
        return jnp.concatenate(
            [jnp.concatenate(lead, axis=1), later_ref[i * frames + LEAD : (i + 1) * frames, :]], axis=0
        )

    transform(columns, table_ref[...], out_ref, spec_ref, inp, frames)


def front(filtered, halo, head, taps, table):
    inp = head.shape[0]
    frames = filtered.shape[0] // inp
    assert 2 * frames == LANES
    chans = table.shape[0] // 2
    return pl.pallas_call(
        front_kernel,
        out_shape=jax.ShapeDtypeStruct((chans * inp, LANES), jnp.bfloat16),
        in_specs=[VMEM] * 5,
        out_specs=VMEM,
        scratch_shapes=[
            pltpu.VMEM((FRAME // LANES, inp * (LEAD + 8), LANES), jnp.float32),
            pltpu.VMEM((chans * (inp + 8), LANES), jnp.float32),
        ],
        compiler_params=params(16),
        name="front",
    )(filtered, halo, head, taps, table)


def tiles_kernel(groups, blocks_time, scale, spec_ref, out_ref, held_ref, sem):
    per = TILE // spec_ref.shape[2]
    half = LANES // 2
    sign = jnp.where(lax.broadcasted_iota(jnp.int32, (TILE, LANES), 1) < half, 1.0, -1.0)
    copies = []
    for chan in range(spec_ref.shape[1]):

        def side(tile):
            return [
                jnp.concatenate([spec_ref[(tile * per + g) * blocks_time + tm, chan] for g in range(per)], axis=0)
                for tm in range(blocks_time)
            ]

        pair = 0
        for a in range(groups // per):
            cols = side(a)
            left = jnp.concatenate(cols, axis=1)
            twisted = jnp.concatenate(
                [(pltpu.roll(c.astype(jnp.float32), half, 1) * sign).astype(jnp.bfloat16) for c in cols], axis=1
            )
            for b in range(a, groups // per):
                right = left if b == a else jnp.concatenate(side(b), axis=1)
                for part, mine in enumerate((left, twisted)):
                    sums = lax.dot_general(mine, right, NT, preferred_element_type=jnp.float32)
                    held_ref[chan, pair, part] = sums * scale
                pair += 1
        copies.append(pltpu.make_async_copy(held_ref.at[chan], out_ref.at[chan], sem.at[chan]))
        copies[-1].start()
    for copy in copies:
        copy.wait()


def tile_sums(spec, groups, blocks_time, scale):
    _, chans, inp, _ = spec.shape
    count = groups * inp // TILE
    shape = (chans, count * (count + 1) // 2, 2, TILE, TILE)
    return pl.pallas_call(
        functools.partial(tiles_kernel, groups, blocks_time, scale),
        out_shape=jax.ShapeDtypeStruct(shape, jnp.float32),
        in_specs=[VMEM],
        out_specs=ANY,
        scratch_shapes=[pltpu.VMEM(shape, jnp.float32), pltpu.SemaphoreType.DMA((chans,))],
        compiler_params=params(32),
        name="tiles",
    )(spec)


def on_device(voltages, pfb_taps):
    inp = voltages.shape[0]
    frames = voltages.shape[1] // FRAME
    groups, blocks_time = lax.axis_size("inputs"), lax.axis_size("tm")
    tail = voltages[:, voltages.shape[1] - (TAPS - 1) * FRAME :]
    halo = lax.ppermute(tail, "tm", [(i, (i + 1) % blocks_time) for i in range(blocks_time)])
    filtered, head = later(voltages, pfb_taps)
    spec = front(filtered, halo, head, pfb_taps, dft_table(F, FRAME))
    turned = lax.all_to_all(spec, ("inputs", "tm"), split_axis=0, concat_axis=0, tiled=True)
    scale = 1.0 / (frames * blocks_time)
    every = groups * blocks_time
    return tile_sums(turned.reshape(every, F // every, inp, LANES), groups, blocks_time, scale)


def solution(mesh):
    return jax.shard_map(
        on_device,
        mesh=mesh,
        in_specs=(P("inputs", "tm"), P()),
        out_specs=P(("inputs", "tm"), None, None, None, None),
        check_vma=False,
    )
```
